256 devices in a mesh: ind: 64 (over z_hi, y, x, core), snp: 4 (over z_lo).
Axes of the slice: x: 4, y: 4, z: 8 (z_hi: 2, z_lo: 4; z = z_hi * 4 + z_lo), core: 2. Of those that a mesh axis runs over, the one named last changes fastest.
Arguments:
- dosages: bfloat16 [11264, 131072], P('ind', 'snp'), may hold values from 0 to 2, as said below
- phenotype: int32 [11264], P('ind'), may hold values 0 or 1
- mean_effect: float32 [131072], P(('snp', 'ind')), may hold values from -3 to 3
- factor: float32 [131072, 256], P(('snp', 'ind')), may hold values from -1 to 1
- log_scale: float32 [131072], P(('snp', 'ind')), may hold values from -1 to 0
- diag_noise: float32 [131072, 128], P(('snp', 'ind')), may hold values from -5 to 5
- base_points: float32 [128, 256], replicated, may hold values from -5 to 5
Outputs:
- grad_mean: float32 [131072], P(('snp', 'ind'))
- grad_factor: float32 [131072, 256], P(('snp', 'ind'))
- grad_log_scale: float32 [131072], P(('snp', 'ind'))
- mean_loglik: float32 [], replicated
- rank_entropy: float32 [], replicated
The draws below stay inside these ranges and needn't reach their ends.
Inputs may be any that keep to these rules, and one draw needn't show every extreme that they name: `dosages`: each entry is an allele count.
All inputs are finite; a program needn't handle non-finite values. No bound on the sum of `phenotype` on one device may be relied on, other than what follows from the above.
Results may differ from the reference program's by a relative error of at most 0.00085.
The reference program's roundings to bfloat16 on the way (of `samples` and `weights`) count: a program that leaves them out, or rounds other values in their place, can miss the bound.
Values may be sent and summed in bfloat16 or wider, within the bound.
No kernel may reach another device: no remote copies, remote signals or barrier semaphores. Data moves between devices by JAX's collectives and lax.ppermute only.
A program may use at most 128 MiB of HBM per device.

```python
import math
import jax
import jax.numpy as jnp
from jax import lax

P_SIZE = 131072
R = 256
S = 128
COHORT_RATIO = 40
N = 11264


def draw_dosages(key, part):
    key_freq, key_draw = jax.random.split(key, 2)
    allele_freq = jax.random.randint(key_freq, (1, P_SIZE), 5, 96)
    digits = jax.random.randint(key_draw, (N, P_SIZE), 0, 10000)
    first = digits // 100 < allele_freq
    second = digits % 100 < allele_freq
    return (first.astype(jnp.float32) + second.astype(jnp.float32)).astype(jnp.bfloat16)


def draw_factor(key, part):
    key_common, key_mixing, key_fresh, key_rows, key_cols = jax.random.split(jax.random.fold_in(key, 17), 5)
    common = jnp.clip(jax.random.normal(key_common, (P_SIZE, 8), jnp.float32), -4.0, 4.0)
    mixing = jnp.clip(jax.random.normal(key_mixing, (8, R), jnp.float32), -4.0, 4.0)
    fresh_noise = jnp.clip(jax.random.normal(key_fresh, (P_SIZE, R), jnp.float32), -5.0, 5.0)
    row_scale = jnp.exp(jax.random.uniform(key_rows, (P_SIZE, 1), jnp.float32, -0.7, 0.7))
    col_scale = jnp.exp(jax.random.uniform(key_cols, (1, R), jnp.float32, -0.7, 0.7))
    shared = common[:, 0:1] * mixing[0:1, :]
    for component in range(1, 8):
        shared = shared + common[:, component:component + 1] * mixing[component:component + 1, :]
    loaded = jnp.sqrt(6.5 / P_SIZE) * row_scale * shared + jnp.sqrt(0.625 / P_SIZE) * fresh_noise
    return jnp.clip(loaded * col_scale, -1.0, 1.0)


def with_ends(result, stream_key, smallest, top_value):
    longest = result.shape.index(max(result.shape))
    spots = []
    for shift in (0, 1):
        where = [jax.random.randint(jax.random.fold_in(stream_key, axis), (), 0, length) for axis, length in enumerate(result.shape)]
        where[longest] = (where[longest] + shift) % result.shape[longest]
        spots.append(tuple(where))
    return result.at[spots[0]].set(smallest).at[spots[1]].set(top_value)


def block_levels(key, extent, pieces, smallest, top_value):
    def one(dim, parts):
        draws = jax.random.uniform(jax.random.fold_in(jax.random.fold_in(key, 6), dim), (parts,), jnp.float32, smallest / len(pieces), top_value / len(pieces))
        return jnp.repeat(jnp.exp(draws), extent[dim] // parts).reshape((-1,) + (1,) * (len(extent) - dim - 1))

    loudness = one(*pieces[0])
    for cut in pieces[1:]:
        loudness = loudness * one(*cut)
    return loudness


def bell_draw(own_key, shape, scale, reach, cuts=(), held_as=jnp.bfloat16):
    result = scale * jax.random.normal(own_key, shape, jnp.float32)
    if cuts:
        result = result * block_levels(own_key, shape, cuts, -0.22, 0.18)
    return jnp.clip(result, -reach, reach).astype(held_as)


def setup_inputs(seed: int = 0) -> dict:
    keys = jax.random.split(jax.random.key(seed), 8)
    return {
        "dosages": draw_dosages(jax.random.fold_in(keys[7], 71), 0),
        "phenotype": with_ends((jax.random.randint(keys[1], (N,), 0, 2) < 1).astype(jnp.int32), jax.random.fold_in(keys[1], 1), 0, 1),
        "mean_effect": bell_draw(keys[2], (P_SIZE,), 0.5, 3.0, ((0, 256),), jnp.float32),
        "factor": draw_factor(jax.random.fold_in(keys[7], 71), 0),
        "log_scale": jnp.clip(-1.0 + 1.0 * jax.random.uniform(keys[4], (P_SIZE,), jnp.float32) ** block_levels(keys[4], (P_SIZE,), ((0, 256),), -0.2, 0.2), -1.0, 0.0),
        "diag_noise": bell_draw(keys[5], (P_SIZE, S), 1.0, 5.0, ((0, 256),), jnp.float32),
        "base_points": bell_draw(keys[6], (S, R), 1.0, 5.0, (), jnp.float32),
    }


def invert_gram(gram_matrix):
    factor_chol = jnp.linalg.cholesky(gram_matrix)
    identity = jnp.eye(gram_matrix.shape[0], dtype=gram_matrix.dtype)
    lower_inv = lax.linalg.triangular_solve(factor_chol, identity, left_side=True, lower=True)
    inverse = jnp.dot(lower_inv.T, lower_inv, precision=lax.Precision.HIGHEST)
    return (factor_chol, inverse)

def reference(dosages, phenotype, mean_effect, factor, log_scale, diag_noise, base_points):
    root_p = math.sqrt(P_SIZE)
    spread = jnp.exp(log_scale)
    low_rank = jnp.dot(factor, base_points.T, precision=lax.Precision.HIGHEST)
    samples = ((mean_effect[:, None] + low_rank + spread[:, None] * diag_noise) / root_p).astype(jnp.bfloat16)
    block_width = math.gcd(P_SIZE, 8192)
    blocks = P_SIZE // block_width

    def add_block(running, block_index):
        columns = lax.dynamic_slice_in_dim(dosages, block_index * block_width, block_width, 1)
        segment = lax.dynamic_slice_in_dim(samples, block_index * block_width, block_width, 0)
        return (running + jnp.dot(columns.astype(jnp.float32), segment.astype(jnp.float32), preferred_element_type=jnp.float32), None)
    logits, _ = lax.scan(add_block, jnp.zeros((N, S), jnp.float32), jnp.arange(blocks, dtype=jnp.int32))
    labels = phenotype.astype(jnp.float32)[:, None]
    mean_loglik = jnp.sum(labels * logits - jax.nn.softplus(logits)) / (N * S)
    weights = (COHORT_RATIO * (labels - jax.nn.sigmoid(logits)) / S).astype(jnp.bfloat16)

    def grad_block(block_index):
        columns = lax.dynamic_slice_in_dim(dosages, block_index * block_width, block_width, 1)
        return lax.dot_general(columns.astype(jnp.float32), weights.astype(jnp.float32), (((0,), (0,)), ((), ())), preferred_element_type=jnp.float32)
    gradient = lax.map(grad_block, jnp.arange(blocks, dtype=jnp.int32)).reshape(P_SIZE, S)
    scaled = factor / spread[:, None]
    identity = jnp.eye(R, dtype=jnp.float32)
    gram_matrix = identity + jnp.dot(scaled.T, scaled, precision=lax.Precision.HIGHEST)
    factor_chol, inverse = invert_gram(gram_matrix)
    rank_entropy = jnp.sum(jnp.log(jnp.diagonal(factor_chol))) / R
    projected = jnp.dot(factor, inverse, precision=lax.Precision.HIGHEST)
    grad_mean = lax.optimization_barrier(jnp.sum(gradient, axis=1)) / root_p - mean_effect
    grad_factor = jnp.dot(gradient, base_points, precision=lax.Precision.HIGHEST) / root_p - factor + projected / (spread * spread)[:, None]
    leverage = lax.optimization_barrier(jnp.sum(projected * factor, axis=1))
    grad_log_scale = spread * lax.optimization_barrier(jnp.sum(gradient * diag_noise, axis=1)) / root_p + 1.0 - spread * spread - leverage / (spread * spread)
    return (grad_mean, grad_factor, grad_log_scale, mean_loglik, rank_entropy)
```

```python
import math

import jax
import jax.numpy as jnp
from jax import lax
from jax.experimental import pallas as pl
from jax.experimental.pallas import tpu as pltpu
from jax.sharding import Mesh
from jax.sharding import PartitionSpec as P

P_SIZE = 131072
R = 256
S = 128
COHORT_RATIO = 40
IND = ("zh", "y", "x", "c")
HIGHEST = lax.Precision.HIGHEST
F32, BF16, F16 = jnp.float32, jnp.bfloat16, jnp.float16
BLOCK = 256
BUNDLE = 8 * BLOCK
VMEM_LIMIT = 48 * 1024 * 1024


def receive(a, axis, k, n):
    return lax.ppermute(a, axis, [((i + k) % n, i) for i in range(n)])


def sum4(a, axis):
    r2, r1, r3 = (receive(a, axis, k, 4) for k in (2, 1, 3))
    return (a + r2) + (r1 + r3)


def extract_body(where, d_ref, out_ref, sem):
    zh, y, x, c = where[0], where[1], where[2], where[3]
    for j in range(8):
        k, half = j // 2, j % 2
        for i in range(8):
            dz, dn = i // 4, i % 4
            dy, dx = (k, dn) if half == 0 else (dn, k)
            chip = (((zh + dz) % 2) * 4 + (y + dy) % 4) * 4 + (x + dx) % 4
            start = pl.multiple_of(chip * 1024 + c * 512 + half * BLOCK, BLOCK)
            pltpu.make_async_copy(
                d_ref.at[:, pl.ds(start, BLOCK)],
                out_ref.at[:, pl.ds((j * 8 + i) * BLOCK, BLOCK)],
                sem,
            ).start()
    pltpu.make_async_copy(out_ref, out_ref, sem).wait()


def extract(dosages, where):
    rows, columns = dosages.shape
    return pl.pallas_call(
        extract_body,
        out_shape=jax.ShapeDtypeStruct((rows, columns // 2), dosages.dtype),
        in_specs=[
            pl.BlockSpec(memory_space=pltpu.SMEM),
            pl.BlockSpec(memory_space=pl.ANY),
        ],
        out_specs=pl.BlockSpec(memory_space=pl.ANY),
        scratch_shapes=[pltpu.SemaphoreType.DMA],
        cost_estimate=pl.CostEstimate(
            flops=0, bytes_accessed=rows * columns * 2, transcendentals=0
        ),
        name="extract",
    )(where, dosages)


def logits_body(n, own_ref, oth_ref, *refs):
    bundles, (in_own, in_oth), (acc_own, acc_oth) = refs[:n], refs[n : n + 2], refs[n + 2 :]
    step = pl.program_id(0)

    @pl.when(step == 0)
    def _():
        acc_own[...] = in_own[...]
        acc_oth[...] = in_oth[...]

    for g in range(n):

        @pl.when(step == g)
        def _():
            block = bundles[g][...]
            acc_own[...] += jnp.dot(own_ref[...], block, preferred_element_type=F32)
            acc_oth[...] += jnp.dot(oth_ref[...], block, preferred_element_type=F32)


def logits_part(own, oth, bundles, first, acc):
    rows = own.shape[0]
    n = len(bundles)
    whole = lambda shape: pl.BlockSpec(shape, lambda g: (0,) * len(shape))
    d_spec = pl.BlockSpec((rows, BUNDLE), lambda g: (0, first + g))
    out = jax.ShapeDtypeStruct((rows, S), F32)
    return pl.pallas_call(
        lambda *refs: logits_body(n, *refs),
        grid=(n,),
        out_shape=(out, out),
        in_specs=[d_spec, d_spec] + [whole((BUNDLE, S))] * n + [whole((rows, S))] * 2,
        out_specs=(whole((rows, S)), whole((rows, S))),
        compiler_params=pltpu.CompilerParams(vmem_limit_bytes=VMEM_LIMIT),
        cost_estimate=pl.CostEstimate(
            flops=4 * rows * S * BUNDLE * n,
            bytes_accessed=n * (rows * BUNDLE * 4 + BUNDLE * S * 2),
            transcendentals=0,
        ),
        name="logits_part",
    )(own, oth, *[b.reshape(BUNDLE, S) for b in bundles], *acc)


def gradient_body(own_ref, oth_ref, w_own, w_oth, out_a, out_b):
    step = pl.program_id(0)
    for g, out in enumerate((out_a, out_b)):

        @pl.when(step == g)
        def _():
            for b in range(8):
                cols = slice(b * BLOCK, (b + 1) * BLOCK)
                part = jnp.dot(w_own[...], own_ref[:, cols], preferred_element_type=F32)
                part += jnp.dot(w_oth[...], oth_ref[:, cols], preferred_element_type=F32)
                out[b] = part


def gradient_part(own, oth, w_own, w_oth, k):
    rows = own.shape[0]
    d_spec = pl.BlockSpec((rows, BUNDLE), lambda g: (0, 2 * k + g))
    w_spec = pl.BlockSpec((S, rows), lambda g: (0, 0))
    out = jax.ShapeDtypeStruct((8, S, BLOCK), F32)
    out_spec = pl.BlockSpec((8, S, BLOCK), lambda g: (0, 0, 0))
    return pl.pallas_call(
        gradient_body,
        grid=(2,),
        out_shape=(out, out),
        in_specs=[d_spec, d_spec, w_spec, w_spec],
        out_specs=(out_spec, out_spec),
        compiler_params=pltpu.CompilerParams(vmem_limit_bytes=VMEM_LIMIT),
        cost_estimate=pl.CostEstimate(
            flops=8 * rows * S * BUNDLE,
            bytes_accessed=rows * BUNDLE * 8 + 16 * S * BLOCK * 4,
            transcendentals=0,
        ),
        name="gradient_part",
    )(own, oth, w_own, w_oth)


def gather_samples(own_rows):
    both = jnp.stack([own_rows, receive(own_rows, "zh", 1, 2)])
    a, b = both[:, :BLOCK], both[:, BLOCK:]
    ax = jnp.stack([a] + [receive(a, "x", k, 4) for k in (1, 2, 3)], axis=1)
    by = jnp.stack([b] + [receive(b, "y", k, 4) for k in (1, 2, 3)], axis=1)
    bundles = [(ax, by)]
    for k in (1, 2, 3):
        bundles.append((receive(ax, "y", k, 4), receive(by, "x", k, 4)))
    return bundles


def reduce_half(pieces, first_axis, second_axis):
    sent = lambda k: pieces[k].astype(F16)
    r1, r2, r3 = (receive(sent(k), first_axis, -k, 4).astype(F32) for k in (1, 2, 3))
    part = ((pieces[0] + r2) + (r1 + r3)).reshape(2, 4, S, BLOCK)
    sent = part[:, 1:].astype(F16)
    r1, r2, r3 = (receive(sent[:, k - 1], second_axis, -k, 4).astype(F32) for k in (1, 2, 3))
    return (part[:, 0] + r2) + (r1 + r3)


def sum_gram(part, c, x):
    half = R // 2
    mine = lax.dynamic_slice_in_dim(part, c * half, half, 0)
    other = lax.dynamic_slice_in_dim(part, (1 - c) * half, half, 0)
    rows = mine + receive(other, "c", 1, 2)
    quarter = half // 4
    piece = lambda k: lax.dynamic_slice_in_dim(rows, ((x - k) % 4) * quarter, quarter, 0)
    r1, r2, r3 = (receive(piece(k), "x", k, 4) for k in (1, 2, 3))
    total = (piece(0) + r2) + (r1 + r3)
    total = sum4(sum4(total, "y"), "snp")
    total = total + receive(total, "zh", 1, 2)
    parts = jnp.stack([total] + [receive(total, "x", k, 4) for k in (1, 2, 3)])
    rows = jnp.roll(parts, x, axis=0).reshape(half, R)
    other = receive(rows, "c", 1, 2)
    return jnp.where(c == 0, jnp.concatenate([rows, other]), jnp.concatenate([other, rows]))


def invert_gram(gram):
    h = R // 2
    eye = jnp.eye(h, dtype=F32)
    dot = lambda a, b: jnp.dot(a, b, precision=HIGHEST)
    solve = lambda l: lax.linalg.triangular_solve(l, eye, left_side=True, lower=True)
    l11 = lax.linalg.cholesky(gram[:h, :h], symmetrize_input=False)
    i11 = solve(l11)
    l21 = dot(gram[h:, :h], i11.T)
    l22 = lax.linalg.cholesky(gram[h:, h:] - dot(l21, l21.T), symmetrize_input=False)
    i22 = solve(l22)
    i21 = -dot(i22, dot(l21, i11))
    top = jnp.concatenate([dot(i11.T, i11) + dot(i21.T, i21), dot(i21.T, i22)], axis=1)
    bottom = jnp.concatenate([dot(i22.T, i21), dot(i22.T, i22)], axis=1)
    inverse = jnp.concatenate([top, bottom], axis=0)
    return jnp.concatenate([jnp.diagonal(l11), jnp.diagonal(l22)]), inverse


def on_device(dosages, phenotype, mean_effect, factor, log_scale, diag_noise, base_points):
    zh, y, x, c = (lax.axis_index(a) for a in IND)
    total_ind = dosages.shape[0] * 64
    root_p = math.sqrt(P_SIZE)
    scale = 2.0 ** math.floor(math.log2(65504 * S / (2 * COHORT_RATIO * total_ind)))

    spread = jnp.exp(log_scale)
    low_rank = jnp.dot(factor, base_points.T, precision=HIGHEST)
    samples = ((mean_effect[:, None] + low_rank + spread[:, None] * diag_noise) / root_p).astype(
        BF16
    )
    where = jnp.stack([zh, y, x, 1 - c]).astype(jnp.int32)
    for_other = extract(dosages, where)
    oth = receive(for_other, "c", 1, 2)
    own = extract(dosages, jnp.stack([zh, y, x, c]).astype(jnp.int32))

    bundles = gather_samples(samples)
    zero = jnp.zeros((dosages.shape[0], S), F32)
    acc = logits_part(own, oth, list(bundles[0]), 0, (zero, zero))
    acc = logits_part(own, oth, [b for k in (1, 2, 3) for b in bundles[k]], 2, acc)

    scaled = factor / spread[:, None]
    gram_part = jnp.dot(scaled.T, scaled, precision=HIGHEST)
    gram = jnp.eye(R, dtype=F32) + sum_gram(gram_part, c, x)

    block_logits = (acc[0] + receive(acc[1], "c", 1, 2)).astype(BF16)
    r1, r2, r3 = (receive(block_logits, "snp", k, 4).astype(F32) for k in (1, 2, 3))
    logits = (block_logits.astype(F32) + r2) + (r1 + r3)
    labels = phenotype.astype(F32)[:, None]
    weights = (COHORT_RATIO * (labels - jax.nn.sigmoid(logits)) / S).astype(BF16)
    w_own = (weights * scale).astype(BF16).T
    w_oth = receive(w_own, "c", 1, 2)
    pieces = [gradient_part(own, oth, w_own, w_oth, k) for k in (0, 1, 2, 3)]
    half_a = reduce_half([p[0] for p in pieces], "y", "x")
    half_b = reduce_half([p[1] for p in pieces], "x", "y")
    both = jnp.concatenate([half_a, half_b], axis=-1)
    gradient = (both[0] + receive(both[1], "zh", 1, 2)) * (1.0 / scale)

    loglik = jnp.full((8, 128), jnp.sum(labels * logits - jax.nn.softplus(logits)))
    loglik = sum4(sum4(loglik, "x"), "y")
    loglik = loglik + receive(loglik, "zh", 1, 2)
    loglik = loglik + receive(loglik, "c", 1, 2)
    mean_loglik = loglik[0, 0] / (total_ind * S)

    diagonal, inverse = invert_gram(gram)
    rank_entropy = jnp.sum(jnp.log(diagonal)) / R
    projected = jnp.dot(factor, inverse, precision=HIGHEST)
    spread_sq = spread * spread
    grad_mean = jnp.sum(gradient, axis=0) / root_p - mean_effect
    grad_factor = (
        lax.dot_general(gradient, base_points, (((0,), (0,)), ((), ())), precision=HIGHEST) / root_p
        - factor
        + projected / spread_sq[:, None]
    )
    leverage = jnp.sum(projected * factor, axis=1)
    grad_log_scale = (
        spread * jnp.sum(gradient * diag_noise.T, axis=0) / root_p
        + 1.0
        - spread_sq
        - leverage / spread_sq
    )
    return (grad_mean, grad_factor, grad_log_scale, mean_loglik, rank_entropy)


def solution(mesh):
    fine = Mesh(mesh.devices.reshape(2, 4, 4, 2, 4), IND + ("snp",))
    rows = ("snp",) + IND
    in_specs = (P(IND, "snp"), P(IND), P(rows), P(rows, None), P(rows), P(rows, None), P())
    out_specs = (P(rows), P(rows, None), P(rows), P(), P())
    return jax.shard_map(
        on_device, mesh=fine, in_specs=in_specs, out_specs=out_specs, check_vma=False
    )
```

```python
import math

import jax
import jax.numpy as jnp
from jax import lax
from jax.experimental import pallas as pl
from jax.experimental.pallas import tpu as pltpu
from jax.sharding import Mesh
from jax.sharding import PartitionSpec as P

P_SIZE = 131072
R = 256
S = 128
COHORT_RATIO = 40
IND = ("zh", "y", "x", "c")
HIGHEST = lax.Precision.HIGHEST
F32, BF16, F16 = jnp.float32, jnp.bfloat16, jnp.float16
BLOCK = 256
BUNDLE = 8 * BLOCK
ORDER = (0, 1, 3, 2)
PLACE = {k: i for i, k in enumerate(ORDER)}
MIB = 1024 * 1024


def receive(a, axis, k, n):
    return lax.ppermute(a, axis, [((i + k) % n, i) for i in range(n)])


def sum4(a, axis, sent=F32):
    r2, r1, r3 = (receive(a.astype(sent), axis, k, 4).astype(F32) for k in (2, 1, 3))
    return (a + r2) + (r1 + r3)


def extract_body(where, d_ref, out_ref, held, sem_in, sem_out):
    zh, y, x, c = where[0], where[1], where[2], where[3]
    for j in range(8):
        k, half = ORDER[j // 2], j % 2
        for i in range(8):
            dn, dz = i // 2, i % 2
            dy, dx = (k, dn) if half == 0 else (dn, k)
            chip = (((zh + dz) % 2) * 4 + (y + dy) % 4) * 4 + (x + dx) % 4
            start = pl.multiple_of(chip * 1024 + c * 512 + half * BLOCK, BLOCK)
            pltpu.make_async_copy(
                d_ref.at[:, pl.ds(start, BLOCK)],
                held.at[:, pl.ds((j * 8 + i) * BLOCK, BLOCK)],
                sem_in.at[j],
            ).start()
    for j in range(8):
        part = pl.ds(j * BUNDLE, BUNDLE)
        pltpu.make_async_copy(held.at[:, part], held.at[:, part], sem_in.at[j]).wait()
        pltpu.make_async_copy(held.at[:, part], out_ref.at[:, part], sem_out.at[j]).start()
    for j in range(8):
        part = pl.ds(j * BUNDLE, BUNDLE)
        pltpu.make_async_copy(held.at[:, part], out_ref.at[:, part], sem_out.at[j]).wait()


def extract(dosages, where):
    rows, columns = dosages.shape
    return pl.pallas_call(
        extract_body,
        out_shape=jax.ShapeDtypeStruct((rows, columns // 2), dosages.dtype),
        in_specs=[
            pl.BlockSpec(memory_space=pltpu.SMEM),
            pl.BlockSpec(memory_space=pltpu.HBM),
        ],
        out_specs=pl.BlockSpec(memory_space=pltpu.HBM),
        scratch_shapes=[
            pltpu.VMEM((rows, columns // 2), dosages.dtype),
            pltpu.SemaphoreType.DMA((8,)),
            pltpu.SemaphoreType.DMA((8,)),
        ],
        compiler_params=pltpu.CompilerParams(vmem_limit_bytes=58 * MIB),
        cost_estimate=pl.CostEstimate(
            flops=0, bytes_accessed=rows * columns * 2, transcendentals=0
        ),
        name="extract",
    )(where, dosages)


def in_hbm(a):
    return pltpu.with_memory_space_constraint(a, pltpu.HBM)


def logits_body(n, own_ref, oth_ref, *refs):
    bundles, (acc_own, acc_oth) = refs[:n], refs[n:]
    step = pl.program_id(0)

    @pl.when(step == 0)
    def _():
        acc_own[...] = jnp.zeros_like(acc_own)
        acc_oth[...] = jnp.zeros_like(acc_oth)

    for g in range(n):

        @pl.when(step == g)
        def _():
            block = bundles[g][...]
            acc_own[...] += jnp.dot(own_ref[...], block, preferred_element_type=F32)
            acc_oth[...] += jnp.dot(oth_ref[...], block, preferred_element_type=F32)


def logits_part(own, oth, bundles, width, first):
    rows = own.shape[0]
    n = len(bundles)
    start = first // width
    whole = lambda shape: pl.BlockSpec(shape, lambda g: (0,) * len(shape))
    d_spec = pl.BlockSpec((rows, width), lambda g: (0, start + g))
    out = jax.ShapeDtypeStruct((rows, S), F32)
    return pl.pallas_call(
        lambda *refs: logits_body(n, *refs),
        grid=(n,),
        out_shape=(out, out),
        in_specs=[d_spec, d_spec] + [whole((width, S))] * n,
        out_specs=(whole((rows, S)), whole((rows, S))),
        compiler_params=pltpu.CompilerParams(vmem_limit_bytes=16 * MIB),
        cost_estimate=pl.CostEstimate(
            flops=4 * rows * S * width * n,
            bytes_accessed=n * (rows * width * 4 + width * S * 2),
            transcendentals=0,
        ),
        name="logits_part",
    )(in_hbm(own), in_hbm(oth), *bundles)


def gradient_body(own_ref, oth_ref, w_own, w_oth, out_a, out_b):
    rows = own_ref.shape[0]
    step = pl.program_id(0)
    for g, out in enumerate((out_a, out_b)):

        @pl.when(step == g)
        def _():
            for b in range(8):
                cols = slice(b * BLOCK, (b + 1) * BLOCK)
                part = jnp.dot(w_own[:, :rows], own_ref[:, cols], preferred_element_type=F32)
                part += jnp.dot(w_oth[:, :rows], oth_ref[:, cols], preferred_element_type=F32)
                out[b] = part


def gradient_part(own, oth, w_own, w_oth, k):
    rows = own.shape[0]
    d_spec = pl.BlockSpec((rows, BUNDLE), lambda g: (0, 2 * PLACE[k] + g))
    w_spec = pl.BlockSpec(w_own.shape, lambda g: (0, 0))
    out = jax.ShapeDtypeStruct((8, S, BLOCK), F32)
    out_spec = pl.BlockSpec((8, S, BLOCK), lambda g: (0, 0, 0))
    return pl.pallas_call(
        gradient_body,
        grid=(2,),
        out_shape=(out, out),
        in_specs=[d_spec, d_spec, w_spec, w_spec],
        out_specs=(out_spec, out_spec),
        compiler_params=pltpu.CompilerParams(vmem_limit_bytes=16 * MIB),
        cost_estimate=pl.CostEstimate(flops=1, bytes_accessed=1, transcendentals=0),
        name="gradient_part",
    )(in_hbm(own), in_hbm(oth), w_own, w_oth)


def split3(v):
    high = lax.reduce_precision(v, 8, 7)
    middle = lax.reduce_precision(v - high, 8, 7)
    low = v - high - middle
    return [p.astype(BF16).reshape(-1, S) for p in (high, middle, low)]


def join3(rows, shape):
    n = rows.shape[0] // 3
    high, middle, low = (rows[i * n : (i + 1) * n].astype(F32) for i in range(3))
    return ((high + middle) + low).reshape(shape)


def quarter_of(rows, i):
    n = rows.shape[1] // 4
    return lax.dynamic_slice_in_dim(rows, (i % 4) * n, n, 1)


def swap_pairs(a, axis):
    return lax.ppermute(a, axis, [(0, 1), (1, 0), (2, 3), (3, 2)])


def direct_sum(part, axis):
    r1, r2, r3 = (receive(part[k].astype(F16), axis, -k, 4).astype(F32) for k in (1, 2, 3))
    return (part[0] + r2) + (r1 + r3)


def eliminate(p):
    n = p.shape[0]
    lane = lax.broadcasted_iota(jnp.int32, (8, n), 1)
    row_id = lax.broadcasted_iota(jnp.int32, (8, n), 0)
    whole = lambda v: jnp.broadcast_to(v, (8, n))
    tiles = [p[8 * i : 8 * i + 8, :] for i in range(n // 8)]
    pivots = jnp.ones((8, n), F32)
    for k in range(n):
        home, at = k // 8, k % 8
        here = lane == k
        columns = {i: whole(tiles[i][:, k : k + 1]) for i in range(home, n // 8)}
        pivot = whole(columns[home][at : at + 1, :])
        row = whole(tiles[home][at : at + 1, :])
        pivots = jnp.where(here, pivot, pivots)
        row = jnp.where(here, 1.0, row) * (1.0 / pivot)
        for i, column in columns.items():
            below = jnp.where(here, 0.0, tiles[i]) - column * row
            tiles[i] = jnp.where(row_id > at, below, tiles[i]) if i == home else below
    done = jnp.concatenate(tiles, axis=0)
    ids = [lax.broadcasted_iota(jnp.int32, (n, n), d) for d in (0, 1)]
    diagonal = jnp.sum(jnp.where(ids[0] == ids[1], done, 0.0), axis=1, keepdims=True)
    unit = jnp.where(ids[1] < ids[0], done, jnp.where(ids[0] == ids[1], 1.0, 0.0))
    return unit * lax.rsqrt(diagonal), pivots


def hdot(a, b):
    return jnp.dot(a, b, precision=HIGHEST, preferred_element_type=F32)


def tdot(a, b, contract):
    return lax.dot_general(
        a, b, ((contract[:1], contract[1:]), ((), ())),
        precision=HIGHEST, preferred_element_type=F32,
    )


def invert_block(gram):
    h = gram.shape[0] // 2
    i11, pivots1 = eliminate(gram[:h, :h])
    l21 = tdot(gram[h:, :h], i11, (1, 1))
    i22, pivots2 = eliminate(gram[h:, h:] - tdot(l21, l21, (1, 1)))
    i21 = -hdot(i22, hdot(l21, i11))
    b21 = tdot(i22, i21, (0, 0))
    b11 = tdot(i11, i11, (0, 0)) + tdot(i21, i21, (0, 0))
    b22 = tdot(i22, i22, (0, 0))
    return (b11, b21, b22), (pivots1, pivots2)


def invert_body(where, near_ref, far_ref, inverse_ref, pivots_ref, gram_ref):
    x, c = where[2], where[3]
    h, quarter = R // 2, R // 8
    neighbour = x + 1 - 2 * (x % 2)
    places = ((near_ref, 0, x), (near_ref, 1, x + 2), (far_ref, 0, neighbour), (far_ref, 1, neighbour + 2))
    for ref, i, place in places:
        for j, core in enumerate((c, 1 - c)):
            row = pl.multiple_of(core * h + (place % 4) * quarter, quarter)
            for lanes in range(2):
                start = ((i * 2 + j) * 2 + lanes) * quarter
                part = slice(lanes * h, (lanes + 1) * h)
                gram_ref[pl.ds(row, quarter), part] = ref[start : start + quarter, :]
    ids = [lax.broadcasted_iota(jnp.int32, (R, R), d) for d in (0, 1)]
    gram = gram_ref[...] + jnp.where(ids[0] == ids[1], 1.0, 0.0)
    (b11, b21, b22), (pivots_ref[0], pivots_ref[1]) = invert_block(gram)
    inverse_ref[:h, :h] = b11
    inverse_ref[h:, :h] = b21
    inverse_ref[:h, h:] = b21.T
    inverse_ref[h:, h:] = b22


def invert_gram(where, near, far):
    vmem = pl.BlockSpec(memory_space=pltpu.VMEM)
    return pl.pallas_call(
        invert_body,
        out_shape=(
            jax.ShapeDtypeStruct((R, R), F32),
            jax.ShapeDtypeStruct((2, 8, R // 2), F32),
        ),
        in_specs=[pl.BlockSpec(memory_space=pltpu.SMEM), vmem, vmem],
        scratch_shapes=[pltpu.VMEM((R, R), F32)],
        compiler_params=pltpu.CompilerParams(vmem_limit_bytes=8 * MIB),
        cost_estimate=pl.CostEstimate(flops=40_000_000, bytes_accessed=2**20, transcendentals=256),
        name="invert_gram",
    )(where, near, far)


def final_body(
    near_ref, far_ref, points_ref, noise_ref, mean_ref, spread_ref, rest_ref, rest_scale_ref,
    mean_out, factor_out, scale_out,
):
    gradient = near_ref[...] + far_ref[...]
    mean_out[...] = jnp.sum(gradient, axis=0, keepdims=True) - mean_ref[...]
    noisy = jnp.sum(gradient * noise_ref[...], axis=0, keepdims=True)
    scale_out[...] = spread_ref[...] * noisy + rest_scale_ref[...]
    product = lax.dot_general(
        gradient, points_ref[...], (((0,), (0,)), ((), ())),
        precision=HIGHEST, preferred_element_type=F32,
    )
    factor_out[...] = product + rest_ref[...]


def final_call(*args):
    rows = args[0].shape[1]
    shapes = ((1, rows), (rows, R), (1, rows))
    return pl.pallas_call(
        final_body,
        out_shape=tuple(jax.ShapeDtypeStruct(v, F32) for v in shapes),
        compiler_params=pltpu.CompilerParams(vmem_limit_bytes=8 * MIB),
        cost_estimate=pl.CostEstimate(flops=2 * rows * R * S, bytes_accessed=2 * MIB, transcendentals=0),
        name="final",
    )(*args)


def on_device(dosages, phenotype, mean_effect, factor, log_scale, diag_noise, base_points):
    zh, y, x, c = (lax.axis_index(a) for a in IND)
    stage = lambda *arrays: lax.optimization_barrier(arrays)
    total_ind = dosages.shape[0] * 64
    root_p = math.sqrt(P_SIZE)
    scale = 2.0 ** math.floor(math.log2(65504 * S / (2 * COHORT_RATIO * total_ind)))
    half = R // 2

    spread = jnp.exp(log_scale)
    low_rank = jnp.dot(factor, base_points.T, precision=HIGHEST)
    samples = ((mean_effect[:, None] + low_rank + spread[:, None] * diag_noise) / root_p).astype(
        BF16
    )
    other_plane = receive(samples, "zh", 1, 2)
    scaled = factor / spread[:, None]
    gram_part = jnp.dot(scaled.T, scaled, precision=HIGHEST)
    gram_part = jnp.stack([gram_part[:, :half], gram_part[:, half:]])
    gram = lax.dynamic_slice_in_dim(gram_part, c * half, half, 1)
    gram_sent = lax.dynamic_slice_in_dim(gram_part, (1 - c) * half, half, 1)
    gram = gram + receive(gram_sent, "c", 1, 2)
    where = jnp.stack([zh, y, x, c]).astype(jnp.int32)
    where_other = jnp.stack([zh, y, x, 1 - c]).astype(jnp.int32)
    samples, other_plane, gram, where_other = stage(samples, other_plane, gram, where_other)

    for_other = extract(dosages, where_other)
    piece = (2, R // 8, half)
    plane_a = jnp.concatenate([samples[:BLOCK], other_plane[:BLOCK]])
    plane_b = jnp.concatenate([samples[BLOCK:], other_plane[BLOCK:]])
    span = 2 * BLOCK
    r1, r2, r3 = (
        receive(jnp.concatenate([plane_a] + split3(quarter_of(gram, x - k))), "x", k, 4)
        for k in (1, 2, 3)
    )
    q1, q2, q3 = (receive(plane_b, "y", k, 4) for k in (1, 2, 3))
    gram = quarter_of(gram, x) + join3(r2[span:], piece)
    gram = gram + (join3(r1[span:], piece) + join3(r3[span:], piece))
    bundle_a = jnp.concatenate([plane_a, r1[:span], r2[:span], r3[:span]] + split3(gram))
    bundle_b = jnp.concatenate([plane_b, q1, q2, q3])
    noise_t = diag_noise.T
    bundle_a, bundle_b, gram, noise_t, for_other = stage(
        bundle_a, bundle_b, gram, noise_t, for_other
    )

    oth = receive(for_other, "c", 1, 2)
    a1, a3 = receive(bundle_a, "y", 1, 4), receive(bundle_a, "y", -1, 4)
    b1, b3 = receive(bundle_b, "x", 1, 4), receive(bundle_b, "x", -1, 4)
    own = extract(dosages, where)
    a1, a3, b1, b3, oth, own = stage(a1, a3, b1, b3, oth, own)

    near = BUNDLE // 2
    far_a = receive(jnp.concatenate([a1[:near], a1[BUNDLE:]]), "y", 1, 4)
    far_b = receive(b1[:near], "x", 1, 4)
    far = [far_a, receive(a3[near:BUNDLE], "y", -1, 4)]
    far += [far_b, receive(b3[near:], "x", -1, 4)]
    acc = logits_part(own, oth, [bundle_a, bundle_b, a1, b1, a3, b3], BUNDLE, 0)
    far, acc = stage(far, acc)

    last = logits_part(own, oth, far, near, 6 * BUNDLE)
    gram, last = stage(gram, last)
    gram = gram + join3(far[0][near:], piece)
    gram = gram + (join3(a1[BUNDLE:], piece) + join3(a3[BUNDLE:], piece))
    block_logits = (acc[0] + last[0]) + receive(acc[1] + last[1], "c", 1, 2)
    gram = gram + receive(gram, "snp", 2, 4)
    block_logits, gram = stage(block_logits.astype(BF16), gram)

    logits = sum4(block_logits.astype(F32), "snp", BF16)
    gram = gram + swap_pairs(gram, "snp")
    labels = phenotype.astype(F32)[:, None]
    weights = (COHORT_RATIO * (labels - jax.nn.sigmoid(logits)) / S).astype(BF16)
    w_own = (weights * scale).astype(BF16).T
    w_own, gram, logits = stage(w_own, gram, logits)

    w_oth = receive(w_own, "c", 1, 2)
    gram = gram + receive(gram, "zh", 1, 2)
    w_oth, gram = stage(w_oth, gram)

    axes = (("y", "x"), ("x", "y"))
    pieces = {2: gradient_part(own, oth, w_own, w_oth, 2)}
    for_ahead, for_behind = [], []
    for p, (axis, _) in zip(pieces[2], axes):
        two = p.astype(F16)
        for_ahead.append(receive(two[:4], axis, -1, 4).astype(F32))
        for_behind.append(receive(two[4:], axis, 1, 4).astype(F32))
    loglik = jnp.full((8, 128), jnp.sum(labels * logits - jax.nn.softplus(logits)))
    small = jnp.concatenate([gram.reshape(-1, half), loglik])
    got = receive(small, "c", 1, 2)
    pieces[1] = gradient_part(own, oth, w_own, w_oth, 1)
    small, got, w_own, pieces = stage(small, got, w_own, pieces)
    small = jnp.concatenate([small[:-8], got[:-8], small[-8:] + got[-8:]])
    got = receive(small, "x", 2, 4)
    pieces[3] = gradient_part(own, oth, w_own, w_oth, 3)
    small, got, w_own, pieces = stage(small, got, w_own, pieces)
    small = jnp.concatenate([small[:-8], got[:-8], small[-8:] + got[-8:]])
    got = swap_pairs(small, "x")
    pieces[0] = gradient_part(own, oth, w_own, w_oth, 0)
    pieces, for_ahead, for_behind, small, got = stage(
        pieces, for_ahead, for_behind, small, got
    )

    loglik = small[-8:] + got[-8:]
    parts = []
    pad = lambda v, before: jnp.pad(v, ((before, 4 - before), (0, 0), (0, 0)))
    for i, (axis, _) in enumerate(axes):
        to_ahead = (pieces[1][i] + pad(for_ahead[i], 0)).astype(F16)
        to_behind = (pieces[3][i] + pad(for_behind[i], 4)).astype(F16)
        r1 = receive(to_ahead, axis, -1, 4).astype(F32)
        r3 = receive(to_behind, axis, 1, 4).astype(F32)
        parts.append((pieces[0][i] + (r1 + r3)).reshape(4, 2, S, BLOCK))
    loglik = loglik + receive(loglik, "y", 2, 4)
    inverted = invert_gram(where, small, got)
    parts, loglik, inverted = stage(parts, loglik, inverted)

    parts = [direct_sum(p, axis) for p, (_, axis) in zip(parts, axes)]
    loglik = loglik + receive(loglik, "zh", 1, 2)
    inverse, pivots = inverted
    parts, loglik, inverse, pivots = stage(parts, loglik, inverse, pivots)

    both = jnp.concatenate(parts, axis=-1)
    far = receive(both[1].astype(F16), "zh", 1, 2)
    both, far = both * (1.0 / (scale * root_p)), far.astype(F32) * (1.0 / (scale * root_p))
    projected = jnp.dot(factor, inverse, precision=HIGHEST)
    spread_sq = spread * spread
    leverage = jnp.sum(projected * factor, axis=1)
    rest = projected / spread_sq[:, None] - factor
    rest_scale = 1.0 - spread_sq - leverage / spread_sq
    rank_entropy = 0.5 * jnp.sum(jnp.log(pivots[:, 0])) / R
    loglik, rest, rest_scale, rank_entropy = stage(loglik, rest, rest_scale, rank_entropy)
    loglik = loglik + swap_pairs(loglik, "y")
    mean_loglik = loglik[0, 0] / (total_ind * S)
    near, far, rest, rest_scale, rank_entropy, mean_loglik = stage(
        both[0], far, rest, rest_scale, rank_entropy, mean_loglik
    )

    row = lambda v: v.reshape(1, -1)
    grad_mean, grad_factor, grad_log_scale = final_call(
        near, far, base_points, noise_t, row(mean_effect), row(spread), rest, row(rest_scale)
    )
    return (
        grad_mean.reshape(-1),
        grad_factor,
        grad_log_scale.reshape(-1),
        mean_loglik,
        rank_entropy,
    )


def solution(mesh):
    fine = Mesh(mesh.devices.reshape(2, 4, 4, 2, 4), IND + ("snp",))
    rows = ("snp",) + IND
    in_specs = (P(IND, "snp"), P(IND), P(rows), P(rows, None), P(rows), P(rows, None), P())
    out_specs = (P(rows), P(rows, None), P(rows), P(), P())
    return jax.shard_map(
        on_device, mesh=fine, in_specs=in_specs, out_specs=out_specs, check_vma=False
    )
```

```python
import math

import jax
import jax.numpy as jnp
from jax import lax
from jax.experimental import pallas as pl
from jax.experimental.pallas import tpu as pltpu
from jax.sharding import Mesh
from jax.sharding import PartitionSpec as P

P_SIZE = 131072
R = 256
S = 128
COHORT_RATIO = 40
IND = ("zh", "y", "x", "c")
HIGHEST = lax.Precision.HIGHEST
F32, BF16, F16 = jnp.float32, jnp.bfloat16, jnp.float16
BLOCK = 256
BUNDLE = 8 * BLOCK
ORDER = (0, 1, 3, 2)
PLACE = {k: i for i, k in enumerate(ORDER)}
MIB = 1024 * 1024


def receive(a, axis, k, n):
    return lax.ppermute(a, axis, [((i + k) % n, i) for i in range(n)])


def sum4(a, axis, sent=F32):
    r2, r1, r3 = (receive(a.astype(sent), axis, k, 4).astype(F32) for k in (2, 1, 3))
    return (a + r2) + (r1 + r3)


def extract_body(where, d_ref, out_ref, held, sem_in, sem_out):
    zh, y, x, c = where[0], where[1], where[2], where[3]
    for j in range(8):
        k, half = ORDER[j // 2], j % 2
        for i in range(8):
            dn, dz = i // 2, i % 2
            dy, dx = (k, dn) if half == 0 else (dn, k)
            chip = (((zh + dz) % 2) * 4 + (y + dy) % 4) * 4 + (x + dx) % 4
            start = pl.multiple_of(chip * 1024 + c * 512 + half * BLOCK, BLOCK)
            pltpu.make_async_copy(
                d_ref.at[:, pl.ds(start, BLOCK)],
                held.at[:, pl.ds((j * 8 + i) * BLOCK, BLOCK)],
                sem_in.at[j],
            ).start()
    for j in range(8):
        part = pl.ds(j * BUNDLE, BUNDLE)
        pltpu.make_async_copy(held.at[:, part], held.at[:, part], sem_in.at[j]).wait()
        pltpu.make_async_copy(held.at[:, part], out_ref.at[:, part], sem_out.at[j]).start()
    for j in range(8):
        part = pl.ds(j * BUNDLE, BUNDLE)
        pltpu.make_async_copy(held.at[:, part], out_ref.at[:, part], sem_out.at[j]).wait()


def extract(dosages, where):
    rows, columns = dosages.shape
    return pl.pallas_call(
        extract_body,
        out_shape=jax.ShapeDtypeStruct((rows, columns // 2), dosages.dtype),
        in_specs=[
            pl.BlockSpec(memory_space=pltpu.SMEM),
            pl.BlockSpec(memory_space=pltpu.HBM),
        ],
        out_specs=pl.BlockSpec(memory_space=pltpu.HBM),
        scratch_shapes=[
            pltpu.VMEM((rows, columns // 2), dosages.dtype),
            pltpu.SemaphoreType.DMA((8,)),
            pltpu.SemaphoreType.DMA((8,)),
        ],
        compiler_params=pltpu.CompilerParams(vmem_limit_bytes=58 * MIB),
        cost_estimate=pl.CostEstimate(
            flops=0, bytes_accessed=rows * columns * 2, transcendentals=0
        ),
        name="extract",
    )(where, dosages)


def in_hbm(a):
    return pltpu.with_memory_space_constraint(a, pltpu.HBM)


def logits_body(n, own_ref, oth_ref, *refs):
    bundles, (acc_own, acc_oth) = refs[:n], refs[n:]
    step = pl.program_id(0)

    @pl.when(step == 0)
    def _():
        acc_own[...] = jnp.zeros_like(acc_own)
        acc_oth[...] = jnp.zeros_like(acc_oth)

    for g in range(n):

        @pl.when(step == g)
        def _():
            block = bundles[g][...]
            acc_own[...] += jnp.dot(own_ref[...], block, preferred_element_type=F32)
            acc_oth[...] += jnp.dot(oth_ref[...], block, preferred_element_type=F32)


def logits_part(own, oth, bundles, width, first):
    rows = own.shape[0]
    n = len(bundles)
    start = first // width
    whole = lambda shape: pl.BlockSpec(shape, lambda g: (0,) * len(shape))
    d_spec = pl.BlockSpec((rows, width), lambda g: (0, start + g))
    out = jax.ShapeDtypeStruct((rows, S), F32)
    return pl.pallas_call(
        lambda *refs: logits_body(n, *refs),
        grid=(n,),
        out_shape=(out, out),
        in_specs=[d_spec, d_spec] + [whole((width, S))] * n,
        out_specs=(whole((rows, S)), whole((rows, S))),
        compiler_params=pltpu.CompilerParams(vmem_limit_bytes=16 * MIB),
        cost_estimate=pl.CostEstimate(
            flops=4 * rows * S * width * n,
            bytes_accessed=n * (rows * width * 4 + width * S * 2),
            transcendentals=0,
        ),
        name="logits_part",
    )(in_hbm(own), in_hbm(oth), *bundles)


def gradient_body(own_ref, oth_ref, w_own, w_oth, out_a, out_b):
    rows = own_ref.shape[0]
    step = pl.program_id(0)
    for g, out in enumerate((out_a, out_b)):

        @pl.when(step == g)
        def _():
            for b in range(8):
                cols = slice(b * BLOCK, (b + 1) * BLOCK)
                part = jnp.dot(w_own[:, :rows], own_ref[:, cols], preferred_element_type=F32)
                part += jnp.dot(w_oth[:, :rows], oth_ref[:, cols], preferred_element_type=F32)
                out[b] = part


def gradient_part(own, oth, w_own, w_oth, k):
    rows = own.shape[0]
    d_spec = pl.BlockSpec((rows, BUNDLE), lambda g: (0, 2 * PLACE[k] + g))
    w_spec = pl.BlockSpec(w_own.shape, lambda g: (0, 0))
    out = jax.ShapeDtypeStruct((8, S, BLOCK), F32)
    out_spec = pl.BlockSpec((8, S, BLOCK), lambda g: (0, 0, 0))
    return pl.pallas_call(
        gradient_body,
        grid=(2,),
        out_shape=(out, out),
        in_specs=[d_spec, d_spec, w_spec, w_spec],
        out_specs=(out_spec, out_spec),
        compiler_params=pltpu.CompilerParams(vmem_limit_bytes=16 * MIB),
        cost_estimate=pl.CostEstimate(flops=1, bytes_accessed=1, transcendentals=0),
        name="gradient_part",
    )(in_hbm(own), in_hbm(oth), w_own, w_oth)


def split3(v):
    high = lax.reduce_precision(v, 8, 7)
    middle = lax.reduce_precision(v - high, 8, 7)
    low = v - high - middle
    return [p.astype(BF16).reshape(-1, S) for p in (high, middle, low)]


def join3(rows, shape):
    n = rows.shape[0] // 3
    high, middle, low = (rows[i * n : (i + 1) * n].astype(F32) for i in range(3))
    return ((high + middle) + low).reshape(shape)


def quarter_of(rows, i):
    n = rows.shape[1] // 4
    return lax.dynamic_slice_in_dim(rows, (i % 4) * n, n, 1)


def swap_pairs(a, axis):
    return lax.ppermute(a, axis, [(0, 1), (1, 0), (2, 3), (3, 2)])


def direct_sum(part, axis):
    r1, r2, r3 = (receive(part[k].astype(F16), axis, -k, 4).astype(F32) for k in (1, 2, 3))
    return (part[0] + r2) + (r1 + r3)


def eliminate(p):
    n = p.shape[0]
    lane = lax.broadcasted_iota(jnp.int32, (1, n), 1)
    finished = []
    for k in range(n):
        at = k % 8
        if at == 0 and k > 0:
            finished.append(p[:8, :])
            p = p[8:, :]
        row_id = lax.broadcasted_iota(jnp.int32, (p.shape[0], 1), 0)
        row, column = p[at : at + 1, :], p[:, k : k + 1]
        new_row = jnp.where(lane == k, 1.0, row) * (1.0 / p[at : at + 1, k : k + 1])
        below = jnp.where(lane == k, 0.0, p) - column * new_row
        p = jnp.where(row_id > at, below, p)
    done = jnp.concatenate(finished + [p], axis=0)
    ids = [lax.broadcasted_iota(jnp.int32, (n, n), d) for d in (0, 1)]
    only = jnp.where(ids[0] == ids[1], done, 0.0)
    diagonal = jnp.sum(only, axis=1, keepdims=True)
    unit = jnp.where(ids[1] < ids[0], done, jnp.where(ids[0] == ids[1], 1.0, 0.0))
    return unit * lax.rsqrt(diagonal), jnp.sum(only, axis=0, keepdims=True)


def hdot(a, b):
    return jnp.dot(a, b, precision=HIGHEST, preferred_element_type=F32)


def tdot(a, b, contract):
    return lax.dot_general(
        a, b, ((contract[:1], contract[1:]), ((), ())),
        precision=HIGHEST, preferred_element_type=F32,
    )


def invert_block(gram):
    h = gram.shape[0] // 2
    i11, pivots1 = eliminate(gram[:h, :h])
    l21 = tdot(gram[h:, :h], i11, (1, 1))
    i22, pivots2 = eliminate(gram[h:, h:] - tdot(l21, l21, (1, 1)))
    i21 = -hdot(i22, hdot(l21, i11))
    b21 = tdot(i22, i21, (0, 0))
    b11 = tdot(i11, i11, (0, 0)) + tdot(i21, i21, (0, 0))
    b22 = tdot(i22, i22, (0, 0))
    return (b11, b21, b22), (pivots1, pivots2)


def invert_body(where, near_ref, far_ref, inverse_ref, pivots_ref, gram_ref):
    x, c = where[2], where[3]
    h, quarter = R // 2, R // 8
    neighbour = x + 1 - 2 * (x % 2)
    places = ((near_ref, 0, x), (near_ref, 1, x + 2), (far_ref, 0, neighbour), (far_ref, 1, neighbour + 2))
    for ref, i, place in places:
        for j, core in enumerate((c, 1 - c)):
            row = pl.multiple_of(core * h + (place % 4) * quarter, quarter)
            for lanes in range(2):
                start = ((i * 2 + j) * 2 + lanes) * quarter
                part = slice(lanes * h, (lanes + 1) * h)
                gram_ref[pl.ds(row, quarter), part] = ref[start : start + quarter, :]
    ids = [lax.broadcasted_iota(jnp.int32, (R, R), d) for d in (0, 1)]
    gram = gram_ref[...] + jnp.where(ids[0] == ids[1], 1.0, 0.0)
    (b11, b21, b22), (pivots_ref[0], pivots_ref[1]) = invert_block(gram)
    inverse_ref[:h, :h] = b11
    inverse_ref[h:, :h] = b21
    inverse_ref[:h, h:] = b21.T
    inverse_ref[h:, h:] = b22


def invert_gram(where, near, far):
    vmem = pl.BlockSpec(memory_space=pltpu.VMEM)
    return pl.pallas_call(
        invert_body,
        out_shape=(
            jax.ShapeDtypeStruct((R, R), F32),
            jax.ShapeDtypeStruct((2, 1, R // 2), F32),
        ),
        in_specs=[pl.BlockSpec(memory_space=pltpu.SMEM), vmem, vmem],
        scratch_shapes=[pltpu.VMEM((R, R), F32)],
        compiler_params=pltpu.CompilerParams(vmem_limit_bytes=8 * MIB),
        cost_estimate=pl.CostEstimate(flops=40_000_000, bytes_accessed=2**20, transcendentals=256),
        name="invert_gram",
    )(where, near, far)


def final_body(
    near_ref, far_ref, points_ref, noise_ref, mean_ref, spread_ref, rest_ref, rest_scale_ref,
    mean_out, factor_out, scale_out,
):
    gradient = near_ref[...] + far_ref[...]
    mean_out[...] = jnp.sum(gradient, axis=0, keepdims=True) - mean_ref[...]
    noisy = jnp.sum(gradient * noise_ref[...], axis=0, keepdims=True)
    scale_out[...] = spread_ref[...] * noisy + rest_scale_ref[...]
    product = lax.dot_general(
        gradient, points_ref[...], (((0,), (0,)), ((), ())),
        precision=HIGHEST, preferred_element_type=F32,
    )
    factor_out[...] = product + rest_ref[...]


def final_call(*args):
    rows = args[0].shape[1]
    shapes = ((1, rows), (rows, R), (1, rows))
    return pl.pallas_call(
        final_body,
        out_shape=tuple(jax.ShapeDtypeStruct(v, F32) for v in shapes),
        compiler_params=pltpu.CompilerParams(vmem_limit_bytes=8 * MIB),
        cost_estimate=pl.CostEstimate(flops=2 * rows * R * S, bytes_accessed=2 * MIB, transcendentals=0),
        name="final",
    )(*args)


def on_device(dosages, phenotype, mean_effect, factor, log_scale, diag_noise, base_points):
    zh, y, x, c = (lax.axis_index(a) for a in IND)
    stage = lambda *arrays: lax.optimization_barrier(arrays)
    total_ind = dosages.shape[0] * 64
    root_p = math.sqrt(P_SIZE)
    scale = 2.0 ** math.floor(math.log2(65504 * S / (2 * COHORT_RATIO * total_ind)))
    half = R // 2

    spread = jnp.exp(log_scale)
    low_rank = jnp.dot(factor, base_points.T, precision=HIGHEST)
    samples = ((mean_effect[:, None] + low_rank + spread[:, None] * diag_noise) / root_p).astype(
        BF16
    )
    other_plane = receive(samples, "zh", 1, 2)
    scaled = factor / spread[:, None]
    gram_part = jnp.dot(scaled.T, scaled, precision=HIGHEST)
    gram_part = jnp.stack([gram_part[:, :half], gram_part[:, half:]])
    gram = lax.dynamic_slice_in_dim(gram_part, c * half, half, 1)
    gram_sent = lax.dynamic_slice_in_dim(gram_part, (1 - c) * half, half, 1)
    gram = gram + receive(gram_sent, "c", 1, 2)
    where = jnp.stack([zh, y, x, c]).astype(jnp.int32)
    where_other = jnp.stack([zh, y, x, 1 - c]).astype(jnp.int32)
    samples, other_plane, gram = stage(samples, other_plane, gram)

    piece = (2, R // 8, half)
    plane_a = jnp.concatenate([samples[:BLOCK], other_plane[:BLOCK]])
    plane_b = jnp.concatenate([samples[BLOCK:], other_plane[BLOCK:]])
    span = 2 * BLOCK
    r1, r2, r3 = (
        receive(jnp.concatenate([plane_a] + split3(quarter_of(gram, x - k))), "x", k, 4)
        for k in (1, 2, 3)
    )
    q1, q2, q3 = (receive(plane_b, "y", k, 4) for k in (1, 2, 3))
    gram = quarter_of(gram, x) + join3(r2[span:], piece)
    gram = gram + (join3(r1[span:], piece) + join3(r3[span:], piece))
    bundle_a = jnp.concatenate([plane_a, r1[:span], r2[:span], r3[:span]] + split3(gram))
    bundle_b = jnp.concatenate([plane_b, q1, q2, q3])
    noise_t = diag_noise.T
    where_other, _, _ = stage(where_other, q1, q2)
    for_other = extract(dosages, where_other)
    bundle_a, bundle_b, gram, noise_t, where, for_other = stage(
        bundle_a, bundle_b, gram, noise_t, where, for_other
    )

    oth = receive(for_other, "c", 1, 2)
    a1, a3 = receive(bundle_a, "y", 1, 4), receive(bundle_a, "y", -1, 4)
    b1, b3 = receive(bundle_b, "x", 1, 4), receive(bundle_b, "x", -1, 4)
    own = extract(dosages, where)
    a1, a3, b1, b3, own = stage(a1, a3, b1, b3, own)

    near = BUNDLE // 2
    far_a = receive(jnp.concatenate([a1[:near], a1[BUNDLE:]]), "y", 1, 4)
    far_b = receive(b1[:near], "x", 1, 4)
    far = [far_a, receive(a3[near:BUNDLE], "y", -1, 4)]
    far += [far_b, receive(b3[near:], "x", -1, 4)]
    acc = logits_part(own, oth, [bundle_a, bundle_b, a1, b1, a3, b3], BUNDLE, 0)
    far, acc = stage(far, acc)

    last = logits_part(own, oth, far, near, 6 * BUNDLE)
    gram, last = stage(gram, last)
    gram = gram + join3(far[0][near:], piece)
    gram = gram + (join3(a1[BUNDLE:], piece) + join3(a3[BUNDLE:], piece))
    block_logits = (acc[0] + last[0]) + receive(acc[1] + last[1], "c", 1, 2)
    gram = gram + receive(gram, "snp", 2, 4)
    block_logits, gram = stage(block_logits.astype(BF16), gram)

    logits = sum4(block_logits.astype(F32), "snp", BF16)
    gram = gram + swap_pairs(gram, "snp")
    labels = phenotype.astype(F32)[:, None]
    weights = (COHORT_RATIO * (labels - jax.nn.sigmoid(logits)) / S).astype(BF16)
    w_own = (weights * scale).astype(BF16).T
    loglik = jnp.full((8, 128), jnp.sum(labels * logits - jax.nn.softplus(logits)))
    w_own, gram, loglik = stage(w_own, gram, loglik)

    w_oth = receive(w_own, "c", 1, 2)
    small = jnp.concatenate([gram.reshape(-1, half), loglik])
    small = small + receive(small, "zh", 1, 2)
    w_oth, small = stage(w_oth, small)

    axes = (("y", "x"), ("x", "y"))
    pieces = {2: gradient_part(own, oth, w_own, w_oth, 2)}
    for_ahead, for_behind = [], []
    for p, (axis, _) in zip(pieces[2], axes):
        two = p.astype(F16)
        for_ahead.append(receive(two[:4], axis, -1, 4).astype(F32))
        for_behind.append(receive(two[4:], axis, 1, 4).astype(F32))
    got = receive(small, "c", 1, 2)
    pieces[1] = gradient_part(own, oth, w_own, w_oth, 1)
    small, got, w_own, pieces = stage(small, got, w_own, pieces)
    small = jnp.concatenate([small[:-8], got[:-8], small[-8:] + got[-8:]])
    got = receive(small, "x", 2, 4)
    pieces[3] = gradient_part(own, oth, w_own, w_oth, 3)
    small, got, w_own, pieces = stage(small, got, w_own, pieces)
    small = jnp.concatenate([small[:-8], got[:-8], small[-8:] + got[-8:]])
    got = swap_pairs(small, "x")
    pieces[0] = gradient_part(own, oth, w_own, w_oth, 0)
    pieces, for_ahead, for_behind, small, got = stage(
        pieces, for_ahead, for_behind, small, got
    )

    loglik = small[-8:] + got[-8:]
    parts = []
    pad = lambda v, before: jnp.pad(v, ((before, 4 - before), (0, 0), (0, 0)))
    for i, (axis, _) in enumerate(axes):
        to_ahead = (pieces[1][i] + pad(for_ahead[i], 0)).astype(F16)
        to_behind = (pieces[3][i] + pad(for_behind[i], 4)).astype(F16)
        r1 = receive(to_ahead, axis, -1, 4).astype(F32)
        r3 = receive(to_behind, axis, 1, 4).astype(F32)
        parts.append((pieces[0][i] + (r1 + r3)).reshape(4, 2, S, BLOCK))
    loglik = loglik + receive(loglik, "y", 2, 4)
    inverted = invert_gram(where, small, got)
    parts, loglik, inverted = stage(parts, loglik, inverted)

    parts = [direct_sum(p, axis) for p, (_, axis) in zip(parts, axes)]
    loglik = loglik + swap_pairs(loglik, "y")
    inverse, pivots = inverted
    parts, loglik, inverse, pivots = stage(parts, loglik, inverse, pivots)

    both = jnp.concatenate(parts, axis=-1)
    far = receive(both[1].astype(F16), "zh", 1, 2)
    both, far = both * (1.0 / (scale * root_p)), far.astype(F32) * (1.0 / (scale * root_p))
    projected = jnp.dot(factor, inverse, precision=HIGHEST)
    spread_sq = spread * spread
    leverage = jnp.sum(projected * factor, axis=1)
    rest = projected / spread_sq[:, None] - factor
    rest_scale = 1.0 - spread_sq - leverage / spread_sq
    rank_entropy = 0.5 * jnp.sum(jnp.log(pivots[:, 0])) / R
    loglik, rest, rest_scale, rank_entropy = stage(loglik, rest, rest_scale, rank_entropy)
    mean_loglik = loglik[0, 0] / (total_ind * S)
    near, far, rest, rest_scale, rank_entropy, mean_loglik = stage(
        both[0], far, rest, rest_scale, rank_entropy, mean_loglik
    )

    row = lambda v: v.reshape(1, -1)
    grad_mean, grad_factor, grad_log_scale = final_call(
        near, far, base_points, noise_t, row(mean_effect), row(spread), rest, row(rest_scale)
    )
    return (
        grad_mean.reshape(-1),
        grad_factor,
        grad_log_scale.reshape(-1),
        mean_loglik,
        rank_entropy,
    )


def solution(mesh):
    fine = Mesh(mesh.devices.reshape(2, 4, 4, 2, 4), IND + ("snp",))
    rows = ("snp",) + IND
    in_specs = (P(IND, "snp"), P(IND), P(rows), P(rows, None), P(rows), P(rows, None), P())
    out_specs = (P(rows), P(rows, None), P(rows), P(), P())
    return jax.shard_map(
        on_device, mesh=fine, in_specs=in_specs, out_specs=out_specs, check_vma=False
    )
```

```python
import math

import jax
import jax.numpy as jnp
from jax import lax
from jax.experimental import pallas as pl
from jax.experimental.pallas import tpu as pltpu
from jax.sharding import Mesh
from jax.sharding import PartitionSpec as P

P_SIZE = 131072
R = 256
S = 128
COHORT_RATIO = 40
IND = ("zh", "y", "x", "c")
HIGHEST = lax.Precision.HIGHEST
F32, BF16, F16 = jnp.float32, jnp.bfloat16, jnp.float16
BLOCK = 256
BUNDLE = 8 * BLOCK
ORDER = (0, 1, 3, 2)
PLACE = {k: i for i, k in enumerate(ORDER)}
MIB = 1024 * 1024


def receive(a, axis, k, n):
    return lax.ppermute(a, axis, [((i + k) % n, i) for i in range(n)])


def sum4(a, axis, sent=F32):
    r2, r1, r3 = (receive(a.astype(sent), axis, k, 4).astype(F32) for k in (2, 1, 3))
    return (a + r2) + (r1 + r3)


def extract_body(where, d_ref, out_ref, held, sem_in, sem_out):
    zh, y, x, c = where[0], where[1], where[2], where[3]
    for j in range(8):
        k, half = ORDER[j // 2], j % 2
        for i in range(8):
            dn, dz = i // 2, i % 2
            dy, dx = (k, dn) if half == 0 else (dn, k)
            chip = (((zh + dz) % 2) * 4 + (y + dy) % 4) * 4 + (x + dx) % 4
            start = pl.multiple_of(chip * 1024 + c * 512 + half * BLOCK, BLOCK)
            pltpu.make_async_copy(
                d_ref.at[:, pl.ds(start, BLOCK)],
                held.at[:, pl.ds((j * 8 + i) * BLOCK, BLOCK)],
                sem_in.at[j],
            ).start()
    for j in range(8):
        part = pl.ds(j * BUNDLE, BUNDLE)
        pltpu.make_async_copy(held.at[:, part], held.at[:, part], sem_in.at[j]).wait()
        pltpu.make_async_copy(held.at[:, part], out_ref.at[:, part], sem_out.at[j]).start()
    for j in range(8):
        part = pl.ds(j * BUNDLE, BUNDLE)
        pltpu.make_async_copy(held.at[:, part], out_ref.at[:, part], sem_out.at[j]).wait()


def extract(dosages, where):
    rows, columns = dosages.shape
    return pl.pallas_call(
        extract_body,
        out_shape=jax.ShapeDtypeStruct((rows, columns // 2), dosages.dtype),
        in_specs=[
            pl.BlockSpec(memory_space=pltpu.SMEM),
            pl.BlockSpec(memory_space=pltpu.HBM),
        ],
        out_specs=pl.BlockSpec(memory_space=pltpu.HBM),
        scratch_shapes=[
            pltpu.VMEM((rows, columns // 2), dosages.dtype),
            pltpu.SemaphoreType.DMA((8,)),
            pltpu.SemaphoreType.DMA((8,)),
        ],
        compiler_params=pltpu.CompilerParams(vmem_limit_bytes=58 * MIB),
        cost_estimate=pl.CostEstimate(
            flops=0, bytes_accessed=rows * columns * 2, transcendentals=0
        ),
        name="extract",
    )(where, dosages)


def in_hbm(a):
    return pltpu.with_memory_space_constraint(a, pltpu.HBM)


def logits_body(n, own_ref, oth_ref, *refs):
    bundles, (acc_own, acc_oth) = refs[:n], refs[n:]
    step = pl.program_id(0)

    @pl.when(step == 0)
    def _():
        acc_own[...] = jnp.zeros_like(acc_own)
        acc_oth[...] = jnp.zeros_like(acc_oth)

    for g in range(n):

        @pl.when(step == g)
        def _():
            block = bundles[g][...]
            acc_own[...] += jnp.dot(own_ref[...], block, preferred_element_type=F32)
            acc_oth[...] += jnp.dot(oth_ref[...], block, preferred_element_type=F32)


def logits_part(own, oth, bundles, width, first):
    rows = own.shape[0]
    n = len(bundles)
    start = first // width
    whole = lambda shape: pl.BlockSpec(shape, lambda g: (0,) * len(shape))
    d_spec = pl.BlockSpec((rows, width), lambda g: (0, start + g))
    out = jax.ShapeDtypeStruct((rows, S), F32)
    return pl.pallas_call(
        lambda *refs: logits_body(n, *refs),
        grid=(n,),
        out_shape=(out, out),
        in_specs=[d_spec, d_spec] + [whole((width, S))] * n,
        out_specs=(whole((rows, S)), whole((rows, S))),
        compiler_params=pltpu.CompilerParams(vmem_limit_bytes=16 * MIB),
        cost_estimate=pl.CostEstimate(
            flops=4 * rows * S * width * n,
            bytes_accessed=n * (rows * width * 4 + width * S * 2),
            transcendentals=0,
        ),
        name="logits_part",
    )(in_hbm(own), in_hbm(oth), *bundles)


def gradient_body(own_ref, oth_ref, w_own, w_oth, out_a, out_b):
    rows = own_ref.shape[0]
    step = pl.program_id(0)
    for g, out in enumerate((out_a, out_b)):

        @pl.when(step == g)
        def _():
            for b in range(8):
                cols = slice(b * BLOCK, (b + 1) * BLOCK)
                part = jnp.dot(w_own[:, :rows], own_ref[:, cols], preferred_element_type=F32)
                part += jnp.dot(w_oth[:, :rows], oth_ref[:, cols], preferred_element_type=F32)
                out[b] = part


def gradient_part(own, oth, w_own, w_oth, k):
    rows = own.shape[0]
    d_spec = pl.BlockSpec((rows, BUNDLE), lambda g: (0, 2 * PLACE[k] + g))
    w_spec = pl.BlockSpec(w_own.shape, lambda g: (0, 0))
    out = jax.ShapeDtypeStruct((8, S, BLOCK), F32)
    out_spec = pl.BlockSpec((8, S, BLOCK), lambda g: (0, 0, 0))
    return pl.pallas_call(
        gradient_body,
        grid=(2,),
        out_shape=(out, out),
        in_specs=[d_spec, d_spec, w_spec, w_spec],
        out_specs=(out_spec, out_spec),
        compiler_params=pltpu.CompilerParams(vmem_limit_bytes=16 * MIB),
        cost_estimate=pl.CostEstimate(
            flops=8 * rows * S * BUNDLE if k == 2 else 1,
            bytes_accessed=rows * BUNDLE * 8 + 16 * S * BLOCK * 4 if k == 2 else 1,
            transcendentals=0,
        ),
        name="gradient_part",
    )(in_hbm(own), in_hbm(oth), w_own, w_oth)


def split3(v):
    high = lax.reduce_precision(v, 8, 7)
    middle = lax.reduce_precision(v - high, 8, 7)
    low = v - high - middle
    return [p.astype(BF16).reshape(-1, S) for p in (high, middle, low)]


def join3(rows, shape):
    n = rows.shape[0] // 3
    high, middle, low = (rows[i * n : (i + 1) * n].astype(F32) for i in range(3))
    return ((high + middle) + low).reshape(shape)


def quarter_of(rows, i):
    n = rows.shape[1] // 4
    return lax.dynamic_slice_in_dim(rows, (i % 4) * n, n, 1)


def swap_pairs(a, axis):
    return lax.ppermute(a, axis, [(0, 1), (1, 0), (2, 3), (3, 2)])


def direct_sum(part, axis):
    r1, r2, r3 = (receive(part[k].astype(F16), axis, -k, 4).astype(F32) for k in (1, 2, 3))
    return (part[0] + r2) + (r1 + r3)


def eliminate(p):
    n = p.shape[0]
    lane = lax.broadcasted_iota(jnp.int32, (1, n), 1)
    finished = []
    for k in range(n):
        at = k % 8
        if at == 0 and k > 0:
            finished.append(p[:8, :])
            p = p[8:, :]
        row_id = lax.broadcasted_iota(jnp.int32, (p.shape[0], 1), 0)
        row, column = p[at : at + 1, :], p[:, k : k + 1]
        new_row = jnp.where(lane == k, 1.0, row) * (1.0 / p[at : at + 1, k : k + 1])
        below = jnp.where(lane == k, 0.0, p) - column * new_row
        p = jnp.where(row_id > at, below, p)
    done = jnp.concatenate(finished + [p], axis=0)
    ids = [lax.broadcasted_iota(jnp.int32, (n, n), d) for d in (0, 1)]
    only = jnp.where(ids[0] == ids[1], done, 0.0)
    diagonal = jnp.sum(only, axis=1, keepdims=True)
    unit = jnp.where(ids[1] < ids[0], done, jnp.where(ids[0] == ids[1], 1.0, 0.0))
    return unit * lax.rsqrt(diagonal), jnp.sum(only, axis=0, keepdims=True)


def hdot(a, b):
    return jnp.dot(a, b, precision=HIGHEST, preferred_element_type=F32)


def tdot(a, b, contract):
    return lax.dot_general(
        a, b, ((contract[:1], contract[1:]), ((), ())),
        precision=HIGHEST, preferred_element_type=F32,
    )


def invert_block(gram):
    h = gram.shape[0] // 2
    i11, pivots1 = eliminate(gram[:h, :h])
    l21 = tdot(gram[h:, :h], i11, (1, 1))
    i22, pivots2 = eliminate(gram[h:, h:] - tdot(l21, l21, (1, 1)))
    i21 = -hdot(i22, hdot(l21, i11))
    b21 = tdot(i22, i21, (0, 0))
    b11 = tdot(i11, i11, (0, 0)) + tdot(i21, i21, (0, 0))
    b22 = tdot(i22, i22, (0, 0))
    return (b11, b21, b22), (pivots1, pivots2)


def invert_body(where, near_ref, far_ref, inverse_ref, pivots_ref, gram_ref):
    x, c = where[2], where[3]
    h, quarter = R // 2, R // 8
    neighbour = x + 1 - 2 * (x % 2)
    places = ((near_ref, 0, x), (near_ref, 1, x + 2), (far_ref, 0, neighbour), (far_ref, 1, neighbour + 2))
    for ref, i, place in places:
        for j, core in enumerate((c, 1 - c)):
            row = pl.multiple_of(core * h + (place % 4) * quarter, quarter)
            for lanes in range(2):
                start = ((i * 2 + j) * 2 + lanes) * quarter
                part = slice(lanes * h, (lanes + 1) * h)
                gram_ref[pl.ds(row, quarter), part] = ref[start : start + quarter, :]
    ids = [lax.broadcasted_iota(jnp.int32, (R, R), d) for d in (0, 1)]
    gram = gram_ref[...] + jnp.where(ids[0] == ids[1], 1.0, 0.0)
    (b11, b21, b22), (pivots_ref[0], pivots_ref[1]) = invert_block(gram)
    inverse_ref[:h, :h] = b11
    inverse_ref[h:, :h] = b21
    inverse_ref[:h, h:] = b21.T
    inverse_ref[h:, h:] = b22


def invert_gram(where, near, far):
    vmem = pl.BlockSpec(memory_space=pltpu.VMEM)
    return pl.pallas_call(
        invert_body,
        out_shape=(
            jax.ShapeDtypeStruct((R, R), F32),
            jax.ShapeDtypeStruct((2, 1, R // 2), F32),
        ),
        in_specs=[pl.BlockSpec(memory_space=pltpu.SMEM), vmem, vmem],
        scratch_shapes=[pltpu.VMEM((R, R), F32)],
        compiler_params=pltpu.CompilerParams(vmem_limit_bytes=8 * MIB),
        cost_estimate=pl.CostEstimate(flops=40_000_000, bytes_accessed=2**20, transcendentals=256),
        name="invert_gram",
    )(where, near, far)


def final_body(
    near_ref, far_ref, points_ref, noise_ref, mean_ref, spread_ref, rest_ref, rest_scale_ref,
    mean_out, factor_out, scale_out,
):
    gradient = near_ref[...] + far_ref[...]
    mean_out[...] = jnp.sum(gradient, axis=0, keepdims=True) - mean_ref[...]
    noisy = jnp.sum(gradient * noise_ref[...], axis=0, keepdims=True)
    scale_out[...] = spread_ref[...] * noisy + rest_scale_ref[...]
    product = lax.dot_general(
        gradient, points_ref[...], (((0,), (0,)), ((), ())),
        precision=HIGHEST, preferred_element_type=F32,
    )
    factor_out[...] = product + rest_ref[...]


def final_call(*args):
    rows = args[0].shape[1]
    shapes = ((1, rows), (rows, R), (1, rows))
    return pl.pallas_call(
        final_body,
        out_shape=tuple(jax.ShapeDtypeStruct(v, F32) for v in shapes),
        compiler_params=pltpu.CompilerParams(vmem_limit_bytes=8 * MIB),
        cost_estimate=pl.CostEstimate(flops=2 * rows * R * S, bytes_accessed=2 * MIB, transcendentals=0),
        name="final",
    )(*args)


def on_device(dosages, phenotype, mean_effect, factor, log_scale, diag_noise, base_points):
    zh, y, x, c = (lax.axis_index(a) for a in IND)
    stage = lambda *arrays: lax.optimization_barrier(arrays)
    total_ind = dosages.shape[0] * 64
    root_p = math.sqrt(P_SIZE)
    scale = 2.0 ** math.floor(math.log2(65504 * S / (2 * COHORT_RATIO * total_ind)))
    half = R // 2

    spread = jnp.exp(log_scale)
    low_rank = jnp.dot(factor, base_points.T, precision=HIGHEST)
    samples = ((mean_effect[:, None] + low_rank + spread[:, None] * diag_noise) / root_p).astype(
        BF16
    )
    other_plane = receive(samples, "zh", 1, 2)
    scaled = factor / spread[:, None]
    gram_part = jnp.dot(scaled.T, scaled, precision=HIGHEST)
    gram_part = jnp.stack([gram_part[:, :half], gram_part[:, half:]])
    gram = lax.dynamic_slice_in_dim(gram_part, c * half, half, 1)
    gram_sent = lax.dynamic_slice_in_dim(gram_part, (1 - c) * half, half, 1)
    gram = gram + receive(gram_sent, "c", 1, 2)
    where = jnp.stack([zh, y, x, c]).astype(jnp.int32)
    where_other = jnp.stack([zh, y, x, 1 - c]).astype(jnp.int32)
    samples, other_plane, gram = stage(samples, other_plane, gram)

    piece = (2, R // 8, half)
    plane_a = jnp.concatenate([samples[:BLOCK], other_plane[:BLOCK]])
    plane_b = jnp.concatenate([samples[BLOCK:], other_plane[BLOCK:]])
    span = 2 * BLOCK
    r1, r2, r3 = (
        receive(jnp.concatenate([plane_a] + split3(quarter_of(gram, x - k))), "x", k, 4)
        for k in (1, 2, 3)
    )
    q1, q2, q3 = (receive(plane_b, "y", k, 4) for k in (1, 2, 3))
    gram = quarter_of(gram, x) + join3(r2[span:], piece)
    gram = gram + (join3(r1[span:], piece) + join3(r3[span:], piece))
    bundle_a = jnp.concatenate([plane_a, r1[:span], r2[:span], r3[:span]] + split3(gram))
    bundle_b = jnp.concatenate([plane_b, q1, q2, q3])
    noise_t = diag_noise.T
    where_other, _, _ = stage(where_other, q1, q2)
    for_other = extract(dosages, where_other)
    bundle_a, bundle_b, gram, noise_t, where, for_other = stage(
        bundle_a, bundle_b, gram, noise_t, where, for_other
    )

    oth = receive(for_other, "c", 1, 2)
    a1, a3 = receive(bundle_a, "y", 1, 4), receive(bundle_a, "y", -1, 4)
    b1, b3 = receive(bundle_b, "x", 1, 4), receive(bundle_b, "x", -1, 4)
    own = extract(dosages, where)
    first = logits_part(own, oth, [bundle_a, bundle_b], BUNDLE, 0)
    a1, a3, b1, b3, own, oth, first = stage(a1, a3, b1, b3, own, oth, first)

    near = BUNDLE // 2
    far_a = receive(jnp.concatenate([a1[:near], a1[BUNDLE:]]), "y", 1, 4)
    far_b = receive(b1[:near], "x", 1, 4)
    far = [far_a, receive(a3[near:BUNDLE], "y", -1, 4)]
    far += [far_b, receive(b3[near:], "x", -1, 4)]
    acc = logits_part(own, oth, [a1, b1, a3, b3], BUNDLE, 2 * BUNDLE)
    acc = [v + w for v, w in zip(first, acc)]
    far, acc = stage(far, acc)

    last = logits_part(own, oth, far, near, 6 * BUNDLE)
    gram, last = stage(gram, last)
    gram = gram + join3(far[0][near:], piece)
    gram = gram + (join3(a1[BUNDLE:], piece) + join3(a3[BUNDLE:], piece))
    block_logits = (acc[0] + last[0]) + receive(acc[1] + last[1], "c", 1, 2)
    gram = gram + receive(gram, "snp", 2, 4)
    block_logits = block_logits.astype(BF16)
    gram, _ = stage(gram, block_logits)

    logits = sum4(block_logits.astype(F32), "snp", BF16)
    gram = gram + swap_pairs(gram, "snp")
    labels = phenotype.astype(F32)[:, None]
    weights = (COHORT_RATIO * (labels - jax.nn.sigmoid(logits)) / S).astype(BF16)
    w_own = (weights * scale).astype(BF16).T
    loglik = jnp.full((8, 128), jnp.sum(labels * logits - jax.nn.softplus(logits)))
    gram, loglik, _ = stage(gram, loglik, w_own)

    w_oth = receive(w_own, "c", 1, 2)
    small = jnp.concatenate([gram.reshape(-1, half), loglik])
    small = small + receive(small, "zh", 1, 2)

    axes = (("y", "x"), ("x", "y"))
    pieces = {2: gradient_part(own, oth, w_own, w_oth, 2)}
    for_ahead, for_behind = [], []
    for p, (axis, _) in zip(pieces[2], axes):
        two = p.astype(F16)
        for_ahead.append(receive(two[:4], axis, -1, 4).astype(F32))
        for_behind.append(receive(two[4:], axis, 1, 4).astype(F32))
    small, w_own, pieces = stage(small, w_own, pieces)
    got = receive(small, "c", 1, 2)
    pieces[1] = gradient_part(own, oth, w_own, w_oth, 1)
    small, got, w_own, pieces = stage(small, got, w_own, pieces)
    small = jnp.concatenate([small[:-8], got[:-8], small[-8:] + got[-8:]])
    got = receive(small, "x", 2, 4)
    pieces[3] = gradient_part(own, oth, w_own, w_oth, 3)
    small, got, w_own, pieces = stage(small, got, w_own, pieces)
    small = jnp.concatenate([small[:-8], got[:-8], small[-8:] + got[-8:]])
    got = swap_pairs(small, "x")
    pieces[0] = gradient_part(own, oth, w_own, w_oth, 0)
    pieces, for_ahead, for_behind, small, got = stage(
        pieces, for_ahead, for_behind, small, got
    )

    loglik = small[-8:] + got[-8:]
    parts = []
    pad = lambda v, before: jnp.pad(v, ((before, 4 - before), (0, 0), (0, 0)))
    for i, (axis, _) in enumerate(axes):
        to_ahead = (pieces[1][i] + pad(for_ahead[i], 0)).astype(F16)
        to_behind = (pieces[3][i] + pad(for_behind[i], 4)).astype(F16)
        r1 = receive(to_ahead, axis, -1, 4).astype(F32)
        r3 = receive(to_behind, axis, 1, 4).astype(F32)
        parts.append((pieces[0][i] + (r1 + r3)).reshape(4, 2, S, BLOCK))
    loglik = loglik + receive(loglik, "y", 2, 4)
    inverted = invert_gram(where, small, got)
    parts, loglik, inverted = stage(parts, loglik, inverted)

    parts = [direct_sum(p, axis) for p, (_, axis) in zip(parts, axes)]
    loglik = loglik + swap_pairs(loglik, "y")
    inverse, pivots = inverted
    parts, loglik, inverse, pivots = stage(parts, loglik, inverse, pivots)

    both = jnp.concatenate(parts, axis=-1)
    far = receive(both[1].astype(F16), "zh", 1, 2)
    both, far = both * (1.0 / (scale * root_p)), far.astype(F32) * (1.0 / (scale * root_p))
    projected = jnp.dot(factor, inverse, precision=HIGHEST)
    spread_sq = spread * spread
    leverage = jnp.sum(projected * factor, axis=1)
    rest = projected / spread_sq[:, None] - factor
    rest_scale = 1.0 - spread_sq - leverage / spread_sq
    rank_entropy = 0.5 * jnp.sum(jnp.log(pivots[:, 0])) / R
    loglik, rest, rest_scale, rank_entropy = stage(loglik, rest, rest_scale, rank_entropy)
    mean_loglik = loglik[0, 0] / (total_ind * S)
    near, far, rest, rest_scale, rank_entropy, mean_loglik = stage(
        both[0], far, rest, rest_scale, rank_entropy, mean_loglik
    )

    row = lambda v: v.reshape(1, -1)
    grad_mean, grad_factor, grad_log_scale = final_call(
        near, far, base_points, noise_t, row(mean_effect), row(spread), rest, row(rest_scale)
    )
    return (
        grad_mean.reshape(-1),
        grad_factor,
        grad_log_scale.reshape(-1),
        mean_loglik,
        rank_entropy,
    )


def solution(mesh):
    fine = Mesh(mesh.devices.reshape(2, 4, 4, 2, 4), IND + ("snp",))
    rows = ("snp",) + IND
    in_specs = (P(IND, "snp"), P(IND), P(rows), P(rows, None), P(rows), P(rows, None), P())
    out_specs = (P(rows), P(rows, None), P(rows), P(), P())
    return jax.shard_map(
        on_device, mesh=fine, in_specs=in_specs, out_specs=out_specs, check_vma=False
    )
```
